32 devices in a mesh: ctx: 16 (over z, y, core), head: 2 (over x).
Axes of the slice: x: 2, y: 2, z: 4, core: 2. Of those that a mesh axis runs over, the one named last changes fastest.
Arguments:
- queries: bfloat16 [4096, 4096], P(('ctx', 'head')), may hold values from -6 to 6
- keys: bfloat16 [4096, 1024], P(('ctx', 'head')), may hold values from -6 to 6
- values: bfloat16 [4096, 1024], P(('ctx', 'head')), may hold values from -6 to 6
- grad_out: bfloat16 [4096, 4096], P(('ctx', 'head')), may hold values from -6 to 6
- doc_ids: int32 [4096], replicated, may hold values from 0 to 3, never falling along the last dimension, each value on 1 to 2048 neighbouring positions
Outputs:
- attended: bfloat16 [4096, 4096], P(('ctx', 'head'))
- grad_queries: bfloat16 [4096, 4096], P(('ctx', 'head'))
- grad_keys: bfloat16 [4096, 1024], P(('ctx', 'head'))
- grad_values: bfloat16 [4096, 1024], P(('ctx', 'head'))
The draws below stay inside these ranges and needn't reach their ends.
Inputs may be any that keep to these rules, and one draw needn't show every extreme that they name: `doc_ids`: document numbers never fall along the row; every document has 1 to 2048 tokens and one has exactly 2048.
All inputs are finite; a program needn't handle non-finite values.
Results may differ from the reference program's by a relative error of at most 0.023.
Values may be sent and summed in bfloat16 or wider, within the bound.
A program may use at most 64 MiB of HBM per device.

```python
import math
import jax
import jax.numpy as jnp
import numpy as np
from jax import lax

QH = 32
KVH = 8
HD = 128
TOK_DEV = 256
DOC_MOST = 2048
TOKENS = 4096
DOCS = 4
DOC_LONG = 2048


def draw_queries(key, part):
    drawn = jnp.clip(jax.random.normal(jax.random.fold_in(key, 11), (TOKENS, QH * HD), jnp.float32), -6.0, 6.0)
    return drawn.astype(jnp.bfloat16)


def draw_keys(key, part):
    drawn = jnp.clip(jax.random.normal(jax.random.fold_in(key, 12), (TOKENS, KVH * HD), jnp.float32), -6.0, 6.0)
    return drawn.astype(jnp.bfloat16)


def steps_of(rng, extent, shards, low, largest):
    def one(dim, shards_of):
        draws = jax.random.uniform(jax.random.fold_in(jax.random.fold_in(rng, 6), dim), (shards_of,), jnp.float32, low / len(shards), largest / len(shards))
        return jnp.repeat(jnp.exp(draws), extent[dim] // shards_of).reshape((-1,) + (1,) * (len(extent) - dim - 1))

    factor_of = one(*shards[0])
    for cut in shards[1:]:
        factor_of = factor_of * one(*cut)
    return factor_of


def length_profile(number_of, total, limit, skew):
    portions = [(1 << 20) // math.isqrt(grade ** skew) + 1 for grade in range(2, number_of + 1)]
    rest, given = total - limit - (number_of - 1), [1] * (number_of - 1)
    while rest > 0:
        candidates = [i for i in range(number_of - 1) if given[i] < limit]
        pool, left = sum([portions[i] for i in candidates]), rest
        for i in candidates:
            addition = min(limit - given[i], max(1, left * portions[i] // pool), rest)
            given[i] = given[i] + addition
            rest = rest - addition
    return np.array([limit] + given)


def ragged_sizes(key, amount, total, limit, slope):
    if amount == 2:
        one = jax.random.randint(key, (), max(1, total - limit), min(limit, total - 1) + 1)
        return jnp.stack([one, total - one])
    tallies = jnp.asarray(length_profile(amount, total, limit, slope), jnp.int32)
    pairs = (amount - 1) // 2
    donor, taker = tallies[1:1 + 2 * pairs:2], tallies[2:2 + 2 * pairs:2]
    slack = jnp.minimum(donor - 1, limit - taker)
    passed = jax.random.randint(jax.random.fold_in(key, 1), (pairs,), 0, 1 << 20) % (slack + 1)
    tallies = tallies.at[1:1 + 2 * pairs:2].set(donor - passed).at[2:2 + 2 * pairs:2].set(taker + passed)
    return tallies[jax.random.permutation(jax.random.fold_in(key, 2), amount)]


def centred(key, shape, width, most, cuts=(), kind=jnp.bfloat16):
    entries = width * jax.random.normal(key, shape, jnp.float32)
    if cuts:
        entries = entries * steps_of(key, shape, cuts, -0.22, 0.18)
    return jnp.clip(entries, -most, most).astype(kind)


def setup_inputs(seed: int = 0) -> dict:
    key_of = jax.random.split(jax.random.key(seed), 6)
    queries = draw_queries(jax.random.fold_in(key_of[5], 71), 0)
    keys = draw_keys(jax.random.fold_in(key_of[5], 71), 0)
    values = centred(key_of[2], (TOKENS, KVH * HD), 1.0, 6.0, ((0, 32),))
    grad_out = centred(key_of[3], (TOKENS, QH * HD), 1.0, 6.0, ((0, 32),))
    doc_ids = jnp.searchsorted(jnp.cumsum(ragged_sizes(key_of[4], DOCS, TOKENS, DOC_LONG, 1)), jnp.arange(TOKENS), side="right").astype(jnp.int32)
    return {"queries": queries, "keys": keys, "values": values, "grad_out": grad_out, "doc_ids": doc_ids}


def reference(queries, keys, values, grad_out, doc_ids):
    softmax_scale = HD ** -0.5
    group_size = QH // KVH
    window = TOK_DEV + DOC_MOST
    padding = jnp.zeros((DOC_MOST, KVH * HD), jnp.bfloat16)
    key_pad = jnp.concatenate((padding, keys), 0)
    value_pad = jnp.concatenate((padding, values), 0)
    docs_all = doc_ids.astype(jnp.int32)
    doc_pad = jnp.concatenate((jnp.full((DOC_MOST,), -1, jnp.int32), docs_all), 0)
    offsets = jnp.arange(window, dtype=jnp.int32)
    row_ids = jnp.arange(TOK_DEV, dtype=jnp.int32)

    def block_step(carried, block_index):
        grad_key_all, grad_value_all = carried
        row_start = (block_index * TOK_DEV).astype(jnp.int32)
        query_blk = lax.dynamic_slice_in_dim(queries, row_start, TOK_DEV, 0).astype(jnp.float32).reshape(TOK_DEV, KVH, group_size, HD)
        grad_blk = lax.dynamic_slice_in_dim(grad_out, row_start, TOK_DEV, 0).astype(jnp.float32).reshape(TOK_DEV, KVH, group_size, HD)
        key_blk = lax.dynamic_slice_in_dim(key_pad, row_start, window, 0).astype(jnp.float32).reshape(window, KVH, HD)
        value_blk = lax.dynamic_slice_in_dim(value_pad, row_start, window, 0).astype(jnp.float32).reshape(window, KVH, HD)
        doc_keys = lax.dynamic_slice_in_dim(doc_pad, row_start, window, 0)
        doc_rows = lax.dynamic_slice_in_dim(docs_all, row_start, TOK_DEV, 0)
        visible = (doc_rows[:, None] == doc_keys[None, :]) & (offsets[None, :] <= row_ids[:, None] + DOC_MOST)
        scores = jnp.einsum("tkgd,wkd->kgtw", query_blk, key_blk) * softmax_scale
        scores = jnp.where(visible, scores, -1e30)
        row_peak = jnp.max(scores, -1, keepdims=True)
        exponent = jnp.where(visible, jnp.exp(scores - row_peak), 0.0)
        row_total = jnp.sum(exponent, -1, keepdims=True)
        weights_low = (exponent / row_total).astype(jnp.bfloat16)
        weights = lax.optimization_barrier(weights_low).astype(jnp.float32)
        attended = jnp.einsum("kgtw,wkd->tkgd", weights, value_blk).astype(jnp.bfloat16)
        grad_weights = jnp.einsum("tkgd,wkd->kgtw", grad_blk, value_blk)
        row_delta = jnp.sum(weights * grad_weights, -1, keepdims=True)
        scores_low = (weights * (grad_weights - row_delta)).astype(jnp.bfloat16)
        grad_scores = lax.optimization_barrier(scores_low).astype(jnp.float32)
        grad_query = (jnp.einsum("kgtw,wkd->tkgd", grad_scores, key_blk) * softmax_scale).astype(jnp.bfloat16)
        key_term = (jnp.einsum("kgtw,tkgd->wkd", grad_scores, query_blk) * softmax_scale).reshape(window, KVH * HD)
        value_term = jnp.einsum("kgtw,tkgd->wkd", weights, grad_blk).reshape(window, KVH * HD)
        grad_key_all = lax.dynamic_update_slice_in_dim(grad_key_all, lax.dynamic_slice_in_dim(grad_key_all, row_start, window, 0) + key_term, row_start, 0)
        grad_value_all = lax.dynamic_update_slice_in_dim(grad_value_all, lax.dynamic_slice_in_dim(grad_value_all, row_start, window, 0) + value_term, row_start, 0)
        return (grad_key_all, grad_value_all), (attended.reshape(TOK_DEV, QH * HD), grad_query.reshape(TOK_DEV, QH * HD))

    initial = (jnp.zeros((TOKENS + DOC_MOST, KVH * HD), jnp.float32), jnp.zeros((TOKENS + DOC_MOST, KVH * HD), jnp.float32))
    sums, outputs = lax.scan(block_step, initial, jnp.arange(TOKENS // TOK_DEV, dtype=jnp.int32))
    attended_all = outputs[0].reshape(TOKENS, QH * HD)
    grad_query_all = outputs[1].reshape(TOKENS, QH * HD)
    return attended_all, grad_query_all, sums[0][DOC_MOST:].astype(jnp.bfloat16), sums[1][DOC_MOST:].astype(jnp.bfloat16)
```

```python
import functools

import jax
import jax.numpy as jnp
from jax import lax
from jax.experimental import pallas as pl
from jax.experimental.pallas import tpu as pltpu
from jax.sharding import PartitionSpec as P

HD = 128
DOC_MOST = 2048
TILE = 256
LOG2E = 1.4426950408889634
MESH = pl.DeviceIdType.MESH


def place(ctx_low, heads):
    ctx, head = lax.axis_index("ctx"), lax.axis_index("head")
    block = ctx // ctx_low
    me = (ctx - block * ctx_low) * heads + head

    def member(number):
        return (block * ctx_low + number // heads, lax.rem(number, heads))

    return ctx, head, block, me, member


def greet(members, ctx, head, ctx_low, has_prev, has_next):
    barrier = pltpu.get_barrier_semaphore()
    for device in members:
        pl.semaphore_signal(barrier, inc=1, device_id=device, device_id_type=MESH)

    @pl.when(has_prev)
    def _():
        pl.semaphore_signal(barrier, inc=1, device_id=(ctx - ctx_low, head), device_id_type=MESH)

    @pl.when(has_next)
    def _():
        pl.semaphore_signal(barrier, inc=1, device_id=(ctx + ctx_low, head), device_id_type=MESH)

    near = has_prev.astype(jnp.int32) + has_next.astype(jnp.int32)
    pl.semaphore_wait(barrier, len(members) + near)


def gather_kernel(
    heads, ctx_low, blocks, distance, q_ref, k_ref, v_ref, g_ref,
    qo_ref, go_ref, band_ref, own_sem, send_sem, recv_sem, hop_send, hop_recv,
):
    group = ctx_low * heads
    rows = q_ref.shape[0]
    q_cols = q_ref.shape[1] // group
    ctx, head, block, me, member = place(ctx_low, heads)
    has_prev, has_next = block > 0, block < blocks - 1
    others = [lax.rem(me + step, group) for step in range(1, group)]
    greet([member(o) for o in others], ctx, head, ctx_low, has_prev, has_next)
    mine = pl.ds(pl.multiple_of(me * rows, rows), rows)
    parts = (
        (k_ref, HD, band_ref.at[distance, 0]),
        (v_ref, HD, band_ref.at[distance, 1]),
        (q_ref, q_cols, qo_ref),
        (g_ref, q_cols, go_ref),
    )

    def piece(ref, width, number):
        return ref.at[:, pl.ds(pl.multiple_of(number * width, width), width)]

    own, copies = [], []
    for a, (src, width, dst) in enumerate(parts):
        local = pltpu.make_async_copy(piece(src, width, me), dst.at[mine], own_sem.at[a])
        local.start()
        own.append(local)
        line = []
        for step, other in enumerate(others):
            copy = pltpu.make_async_remote_copy(
                src_ref=piece(src, width, other), dst_ref=dst.at[mine],
                send_sem=send_sem.at[a, step], recv_sem=recv_sem.at[a, step],
                device_id=member(other), device_id_type=MESH,
            )
            copy.start()
            line.append(copy)
        copies.append(line)

    def hop(step, c):
        return pltpu.make_async_remote_copy(
            src_ref=band_ref.at[distance - step, c], dst_ref=band_ref.at[distance - step - 1, c],
            send_sem=hop_send.at[step, c], recv_sem=hop_recv.at[step, c],
            device_id=(ctx + ctx_low, head), device_id_type=MESH,
        )

    for step in range(distance):
        for c in range(2):
            if step == 0:
                own[c].wait()
                for copy in copies[c]:
                    copy.wait_recv()
            else:
                @pl.when(block - step >= 0)
                def _():
                    hop(step - 1, c).wait_recv()

            @pl.when((block - step >= 0) & has_next)
            def _():
                hop(step, c).start()

    for a in range(2, 4):
        own[a].wait()
        for copy in copies[a]:
            copy.wait_recv()
    for line in copies:
        for copy in line:
            copy.wait_send()
    for c in range(2):
        @pl.when(block - distance >= 0)
        def _():
            hop(distance - 1, c).wait_recv()

        for step in range(distance):
            @pl.when((block - step >= 0) & has_next)
            def _():
                hop(step, c).wait_send()


def return_kernel(
    heads, ctx_low, blocks, distance, a_ref, d_ref, part_ref,
    ao_ref, do_ref, ko_ref, vo_ref, sums, landed, own_sem, send_sem, recv_sem, hop_send, hop_recv,
):
    group = ctx_low * heads
    rows = ao_ref.shape[0]
    q_cols = a_ref.shape[1]
    ctx, head, block, me, member = place(ctx_low, heads)
    has_prev, has_next = block > 0, block < blocks - 1
    others = [lax.rem(me + step, group) for step in range(1, group)]
    greet([member(o) for o in others], ctx, head, ctx_low, has_prev, has_next)

    def hop(step, c):
        source = part_ref.at[0, c] if step == 0 else sums.at[step - 1, c]
        return pltpu.make_async_remote_copy(
            src_ref=source, dst_ref=landed.at[step, c],
            send_sem=hop_send.at[step, c], recv_sem=hop_recv.at[step, c],
            device_id=(ctx - ctx_low, head), device_id_type=MESH,
        )

    def pieces(number):
        return pl.ds(pl.multiple_of(number * rows, rows), rows)

    own, copies = [], []

    def send(a, src, width, dst):
        column = pl.ds(pl.multiple_of(me * width, width), width)
        local = pltpu.make_async_copy(src.at[pieces(me)], dst.at[:, column], own_sem.at[a])
        local.start()
        own.append(local)
        for step, other in enumerate(others):
            copy = pltpu.make_async_remote_copy(
                src_ref=src.at[pieces(other)], dst_ref=dst.at[:, column],
                send_sem=send_sem.at[a, step], recv_sem=recv_sem.at[a, step],
                device_id=member(other), device_id_type=MESH,
            )
            copy.start()
            copies.append(copy)

    for c in range(2):
        @pl.when(block - distance >= 0)
        def _():
            hop(0, c).start()

    send(0, a_ref, q_cols, ao_ref)
    send(1, d_ref, q_cols, do_ref)

    for step in range(1, distance + 1):
        valid = block - (distance - step) >= 0
        for c in range(2):
            @pl.when(valid & has_next)
            def _():
                hop(step - 1, c).wait_recv()
                both = part_ref[step, c].astype(jnp.float32) + landed[step - 1, c].astype(jnp.float32)
                sums[step - 1, c] = both.astype(jnp.bfloat16)

            @pl.when(valid & jnp.logical_not(has_next))
            def _():
                sums[step - 1, c] = part_ref[step, c]

            if step < distance:
                @pl.when(valid)
                def _():
                    hop(step, c).start()

    send(2, sums.at[distance - 1, 0], HD, ko_ref)
    send(3, sums.at[distance - 1, 1], HD, vo_ref)
    for local in own:
        local.wait()
    for copy in copies:
        copy.wait()
    for c in range(2):
        for step in range(distance):
            @pl.when(block - (distance - step) >= 0)
            def _():
                hop(step, c).wait_send()


def attend_kernel(
    distance, scale, sc_ref, start_ref, q_ref, g_ref, band_ref, att_ref, dq_ref, part_ref,
    acc, kept, qc, qt, gc, gt, peak, total, ot, dqt, kt, vt,
):
    tokens = q_ref.shape[0]
    share = q_ref.shape[1] // HD
    factor = scale * LOG2E
    per_block = tokens // TILE
    base = sc_ref[0]
    first_token = base - distance * tokens
    tiles = tokens // TILE

    acc[...] = jnp.zeros_like(acc)

    def turn(slot, _):
        for t in range(per_block):
            kt[slot * per_block + t] = band_ref[slot, 0, t * TILE:(t + 1) * TILE, :].T
            vt[slot * per_block + t] = band_ref[slot, 1, t * TILE:(t + 1) * TILE, :].T
        return 0

    lax.fori_loop(0, distance + 1, turn, 0)

    def key_tile(kb, c):
        slot = kb // per_block
        offset = pl.multiple_of((kb - slot * per_block) * TILE, TILE)
        return band_ref[slot, c, pl.ds(offset, TILE), :]

    def fold(x, op):
        return op(x.reshape(TILE // 8, 8, TILE), 0)

    def one_tile(i, _):
        row = pl.multiple_of(i * TILE, TILE)
        here = pl.ds(row, TILE)
        low, high = sc_ref[1 + 2 * i], sc_ref[2 + 2 * i]
        kb0 = (low - first_token) // TILE
        kb1 = distance * per_block + i
        for h in range(share):
            span = slice(h * TILE, (h + 1) * TILE)
            head = slice(h * HD, (h + 1) * HD)
            qc[span, :] = q_ref[here, head]
            gc[span, :] = g_ref[here, head]
            qt[:, span] = q_ref[here, head].T
            gt[:, span] = g_ref[here, head].T
        peak[...] = jnp.full_like(peak, -1e30)
        total[...] = jnp.zeros_like(total)
        ot[...] = jnp.zeros_like(ot)
        dqt[...] = jnp.zeros_like(dqt)
        starts = start_ref[:, here]

        def score(kb, _):
            keys = key_tile(kb, 0)
            tile_token = first_token + kb * TILE
            masked = (kb == kb1) | (high > tile_token)

            @pl.when(masked)
            def _():
                col = tile_token + lax.broadcasted_iota(jnp.int32, (TILE, TILE), 0)
                token = base + row + lax.broadcasted_iota(jnp.int32, (TILE, TILE), 1)
                seen = (col >= starts) & (col <= token)
                for h in range(share):
                    span = slice(h * TILE, (h + 1) * TILE)
                    s = jnp.dot(keys, qt[:, span], preferred_element_type=jnp.float32)
                    s = jnp.where(seen, s, -1e30)
                    kept[kb - kb0, :, span] = s
                    peak[:, span] = jnp.maximum(peak[:, span], fold(s, jnp.max))

            @pl.when(jnp.logical_not(masked))
            def _():
                for h in range(share):
                    span = slice(h * TILE, (h + 1) * TILE)
                    s = jnp.dot(keys, qt[:, span], preferred_element_type=jnp.float32)
                    kept[kb - kb0, :, span] = s
                    peak[:, span] = jnp.maximum(peak[:, span], fold(s, jnp.max))

            return 0

        lax.fori_loop(kb0, kb1 + 1, score, 0)
        top = jnp.max(peak[...], 0, keepdims=True) * factor

        def forward(kb, _):
            values_t = vt[kb]
            for h in range(share):
                span = slice(h * TILE, (h + 1) * TILE)
                p = jnp.exp2(kept[kb - kb0, :, span] * factor - top[:, span])
                kept[kb - kb0, :, span] = p
                total[:, span] += fold(p, jnp.sum)
                ot[:, span] += jnp.dot(
                    values_t, p.astype(jnp.bfloat16), preferred_element_type=jnp.float32
                )
            return 0

        lax.fori_loop(kb0, kb1 + 1, forward, 0)
        inverse = 1.0 / jnp.sum(total[...], 0, keepdims=True)
        out = ot[...] * inverse
        delta = jnp.sum(out * gt[...].astype(jnp.float32), 0, keepdims=True)
        for h in range(share):
            span = slice(h * TILE, (h + 1) * TILE)
            att_ref[here, h * HD:(h + 1) * HD] = out[:, span].T.astype(jnp.bfloat16)

        def backward(kb, _):
            values = key_tile(kb, 1)
            keys_t = kt[kb]
            dv = jnp.zeros((TILE, HD), jnp.float32)
            dk = jnp.zeros((TILE, HD), jnp.float32)
            for h in range(share):
                span = slice(h * TILE, (h + 1) * TILE)
                w = kept[kb - kb0, :, span] * inverse[:, span]
                dp = jnp.dot(values, gt[:, span], preferred_element_type=jnp.float32)
                ds = (w * (dp - delta[:, span])).astype(jnp.bfloat16)
                dv += jnp.dot(
                    w.astype(jnp.bfloat16), gc[span, :], preferred_element_type=jnp.float32
                )
                dk += jnp.dot(ds, qc[span, :], preferred_element_type=jnp.float32)
                dqt[:, span] += jnp.dot(keys_t, ds, preferred_element_type=jnp.float32)
            where = pl.ds(pl.multiple_of(kb * TILE, TILE), TILE)
            acc[0, where, :] += dk
            acc[1, where, :] += dv
            return 0

        lax.fori_loop(kb0, kb1 + 1, backward, 0)
        for h in range(share):
            span = slice(h * TILE, (h + 1) * TILE)
            dq_ref[here, h * HD:(h + 1) * HD] = (dqt[:, span] * scale).T.astype(jnp.bfloat16)
        return 0

    lax.fori_loop(0, tiles, one_tile, 0)
    for slot in range(distance + 1):
        span = slice(slot * tokens, (slot + 1) * tokens)
        part_ref[slot, 0] = (acc[0, span, :] * scale).astype(jnp.bfloat16)
        part_ref[slot, 1] = acc[1, span, :].astype(jnp.bfloat16)


def per_device(queries, keys, values, grad_out, doc_ids):
    heads = lax.axis_size("head")
    peers = lax.axis_size("ctx")
    rows = queries.shape[0]
    kv_heads = keys.shape[1] // HD
    q_heads = queries.shape[1] // HD
    share = q_heads // kv_heads
    ctx_low = kv_heads // heads
    blocks = peers // ctx_low
    tokens = rows * kv_heads
    distance = DOC_MOST // tokens
    group = kv_heads
    bf16, f32 = jnp.bfloat16, jnp.float32
    vmem = pl.BlockSpec(memory_space=pltpu.VMEM)
    smem = pl.BlockSpec(memory_space=pltpu.SMEM)
    dma = pltpu.SemaphoreType.DMA
    limit = 60 * 1024 * 1024

    q_all, g_all, band = pl.pallas_call(
        functools.partial(gather_kernel, heads, ctx_low, blocks, distance),
        out_shape=(
            jax.ShapeDtypeStruct((tokens, share * HD), bf16),
            jax.ShapeDtypeStruct((tokens, share * HD), bf16),
            jax.ShapeDtypeStruct((distance + 1, 2, tokens, HD), bf16),
        ),
        in_specs=[vmem] * 4,
        out_specs=(vmem,) * 3,
        scratch_shapes=[
            dma((4,)), dma((4, group - 1)), dma((4, group - 1)),
            dma((distance, 2)), dma((distance, 2)),
        ],
        compiler_params=pltpu.CompilerParams(
            collective_id=1, has_side_effects=True, vmem_limit_bytes=limit
        ),
        name="gather",
    )(queries, keys, values, grad_out)

    block = lax.axis_index("ctx") // ctx_low
    base = block * tokens
    padded = jnp.concatenate((jnp.full((distance * tokens,), -1, jnp.int32), doc_ids), 0)
    window = lax.dynamic_slice_in_dim(padded, base, (distance + 1) * tokens, 0)
    mine = lax.dynamic_slice_in_dim(doc_ids, base, tokens, 0)
    starts = base - distance * tokens + jnp.sum(
        (window[:, None] < mine[None, :]).astype(jnp.int32), 0, dtype=jnp.int32
    )
    tiles = starts.reshape(-1, TILE)
    scalars = jnp.concatenate(
        (base[None].astype(jnp.int32), jnp.stack((tiles[:, 0], tiles[:, -1]), 1).reshape(-1))
    )
    span = share * TILE
    all_tiles = (distance + 1) * tokens // TILE
    attended, grad_query, part = pl.pallas_call(
        functools.partial(attend_kernel, distance, HD ** -0.5),
        out_shape=(
            jax.ShapeDtypeStruct((tokens, share * HD), bf16),
            jax.ShapeDtypeStruct((tokens, share * HD), bf16),
            jax.ShapeDtypeStruct((distance + 1, 2, tokens, HD), bf16),
        ),
        in_specs=[smem, vmem, vmem, vmem, vmem],
        out_specs=(vmem,) * 3,
        scratch_shapes=[
            pltpu.VMEM((2, (distance + 1) * tokens, HD), f32),
            pltpu.VMEM((DOC_MOST // TILE + 1, TILE, span), f32),
            pltpu.VMEM((span, HD), bf16),
            pltpu.VMEM((HD, span), bf16),
            pltpu.VMEM((span, HD), bf16),
            pltpu.VMEM((HD, span), bf16),
            pltpu.VMEM((8, span), f32),
            pltpu.VMEM((8, span), f32),
            pltpu.VMEM((HD, span), f32),
            pltpu.VMEM((HD, span), f32),
            pltpu.VMEM((all_tiles, HD, TILE), bf16),
            pltpu.VMEM((all_tiles, HD, TILE), bf16),
        ],
        compiler_params=pltpu.CompilerParams(vmem_limit_bytes=limit),
        name="attend",
    )(scalars, starts[None, :], q_all, g_all, band)

    return pl.pallas_call(
        functools.partial(return_kernel, heads, ctx_low, blocks, distance),
        out_shape=(
            jax.ShapeDtypeStruct(queries.shape, bf16),
            jax.ShapeDtypeStruct(queries.shape, bf16),
            jax.ShapeDtypeStruct(keys.shape, bf16),
            jax.ShapeDtypeStruct(keys.shape, bf16),
        ),
        in_specs=[vmem] * 3,
        out_specs=(vmem,) * 4,
        scratch_shapes=[
            pltpu.VMEM((distance, 2, tokens, HD), bf16),
            pltpu.VMEM((distance, 2, tokens, HD), bf16),
            dma((4,)), dma((4, group - 1)), dma((4, group - 1)),
            dma((distance, 2)), dma((distance, 2)),
        ],
        compiler_params=pltpu.CompilerParams(
            collective_id=2, has_side_effects=True, vmem_limit_bytes=limit
        ),
        name="give_back",
    )(attended, grad_query, part)


def solution(mesh):
    spec = P(("ctx", "head"), None)
    return jax.shard_map(
        per_device,
        mesh=mesh,
        in_specs=(spec, spec, spec, spec, P()),
        out_specs=(spec, spec, spec, spec),
        check_vma=False,
    )
```

```python
import functools

import jax
import jax.numpy as jnp
from jax import lax
from jax.experimental import pallas as pl
from jax.experimental.pallas import tpu as pltpu
from jax.sharding import PartitionSpec as P

HD = 128
DOC_MOST = 2048
TILE = 256
LOG2E = 1.4426950408889634
MESH = pl.DeviceIdType.MESH


def place(ctx_low, heads):
    ctx, head = lax.axis_index("ctx"), lax.axis_index("head")
    block = ctx // ctx_low
    me = (ctx - block * ctx_low) * heads + head

    def member(number):
        return (block * ctx_low + number // heads, lax.rem(number, heads))

    return ctx, head, block, me, member


def greet(members, ctx, head, ctx_low, has_prev, has_next):
    barrier = pltpu.get_barrier_semaphore()
    for device in members:
        pl.semaphore_signal(barrier, inc=1, device_id=device, device_id_type=MESH)

    @pl.when(has_prev)
    def _():
        pl.semaphore_signal(barrier, inc=1, device_id=(ctx - ctx_low, head), device_id_type=MESH)

    @pl.when(has_next)
    def _():
        pl.semaphore_signal(barrier, inc=1, device_id=(ctx + ctx_low, head), device_id_type=MESH)

    near = has_prev.astype(jnp.int32) + has_next.astype(jnp.int32)
    pl.semaphore_wait(barrier, len(members) + near)


def fused_kernel(
    heads, ctx_low, blocks, distance, scale,
    start_ref, q_in, k_in, v_in, g_in,
    ao_ref, do_ref, ko_ref, vo_ref,
    qo, go, band, acc, kept, qt, gt, peak, total, ot, dqt, kt, vt, inv, delta,
    att, dq, sums, landed,
    own_sem, send_sem, recv_sem, in_send, in_recv, out_send, out_recv,
):
    group = ctx_low * heads
    rows = q_in.shape[0]
    q_cols = q_in.shape[1] // group
    tokens = qo.shape[0]
    share = q_cols // HD
    factor = scale * LOG2E
    per_block = tokens // TILE
    reach = distance * per_block + 1
    ctx, head, block, me, member = place(ctx_low, heads)
    has_prev, has_next = block > 0, block < blocks - 1
    others = [lax.rem(me + step, group) for step in range(1, group)]
    greet([member(o) for o in others], ctx, head, ctx_low, has_prev, has_next)
    mine = pl.ds(pl.multiple_of(me * rows, rows), rows)
    base = block * tokens
    first_token = base - distance * tokens
    first_kb = jnp.maximum(distance - block, 0) * per_block

    def columns(width, number):
        return pl.ds(pl.multiple_of(number * width, width), width)

    def swap(a, pick_src, pick_dst):
        local = pltpu.make_async_copy(pick_src(me), pick_dst(me), own_sem.at[a])
        local.start()
        line = []
        for step, other in enumerate(others):
            copy = pltpu.make_async_remote_copy(
                src_ref=pick_src(other), dst_ref=pick_dst(me),
                send_sem=send_sem.at[a, step], recv_sem=recv_sem.at[a, step],
                device_id=member(other), device_id_type=MESH,
            )
            copy.start()
            line.append(copy)
        return local, line

    def swap_in(a, src, width, dst):
        return swap(a, lambda n: src.at[:, columns(width, n)], lambda n: dst.at[mine])

    def swap_out(a, src, width, dst):
        return swap(
            a,
            lambda n: src.at[pl.ds(pl.multiple_of(n * rows, rows), rows)],
            lambda n: dst.at[:, columns(width, n)],
        )

    def settle(pair):
        pair[0].wait()
        for copy in pair[1]:
            copy.wait_recv()

    def hop_in(step, c):
        return pltpu.make_async_remote_copy(
            src_ref=band.at[distance - step, c], dst_ref=band.at[distance - step - 1, c],
            send_sem=in_send.at[step, c], recv_sem=in_recv.at[step, c],
            device_id=(ctx + ctx_low, head), device_id_type=MESH,
        )

    def hop_out(step, c):
        return pltpu.make_async_remote_copy(
            src_ref=sums.at[step, c], dst_ref=landed.at[step, c],
            send_sem=out_send.at[step, c], recv_sem=out_recv.at[step, c],
            device_id=(ctx - ctx_low, head), device_id_type=MESH,
        )

    kv_swap = [
        swap_in(0, k_in, HD, band.at[distance, 0]),
        swap_in(1, v_in, HD, band.at[distance, 1]),
    ]
    qg_swap = [swap_in(2, q_in, q_cols, qo), swap_in(3, g_in, q_cols, go)]
    acc[...] = jnp.zeros_like(acc)
    dqt[...] = jnp.zeros_like(dqt)
    peak[...] = jnp.full_like(peak, -1e30)
    for c in range(2):
        settle(kv_swap[c])

        @pl.when(has_next)
        def _():
            hop_in(0, c).start()

    for pair in qg_swap:
        settle(pair)

    spans = [slice(h * TILE, (h + 1) * TILE) for h in range(share)]
    cols = [slice(h * HD, (h + 1) * HD) for h in range(share)]

    def tile_rows(i):
        return pl.ds(pl.multiple_of(i * TILE, TILE), TILE)

    def turn_rows(i, _):
        here = tile_rows(i)
        for h in range(share):
            qt[i, :, spans[h]] = qo[here, cols[h]].T
            gt[i, :, spans[h]] = go[here, cols[h]].T
        return 0

    lax.fori_loop(0, per_block, turn_rows, 0)

    def fold(x, op):
        return op(x.reshape(TILE // 8, 8, TILE), 0)

    def score_slot(n, _):
        slot = distance - n

        @pl.when(block - n >= 0)
        def _():
            for c in range(2):
                @pl.when(n > 0)
                def _():
                    hop_in(n - 1, c).wait_recv()

                @pl.when((n > 0) & (n < distance) & has_next)
                def _():
                    hop_in(n, c).start()

            def key_step(t, _):
                kb = slot * per_block + t
                here = tile_rows(t)
                keys = band[slot, 0, here, :]
                kt[kb] = keys.T
                vt[kb] = band[slot, 1, here, :].T
                tile_token = first_token + kb * TILE
                col = tile_token + lax.broadcasted_iota(jnp.int32, (TILE, TILE), 0)

                def row_step(i, _):
                    starts = start_ref[i]
                    token = base + i * TILE + lax.broadcasted_iota(jnp.int32, (TILE, TILE), 1)
                    seen = (col >= starts) & (col <= token)
                    for h in range(share):
                        s = jnp.dot(keys, qt[i, :, spans[h]], preferred_element_type=jnp.float32)
                        s = jnp.where(seen, s, -1e30)
                        kept[i, kb - i, :, spans[h]] = s
                        peak[i, :, spans[h]] = jnp.maximum(peak[i, :, spans[h]], fold(s, jnp.max))
                    return 0

                lax.fori_loop(
                    jnp.maximum(kb - reach + 1, 0), jnp.minimum(kb + 1, per_block), row_step, 0
                )
                return 0

            lax.fori_loop(0, per_block, key_step, 0)

        return 0

    lax.fori_loop(0, distance + 1, score_slot, 0)

    def forward_tile(i, _):
        here = tile_rows(i)
        top = jnp.max(peak[i], 0, keepdims=True) * factor
        total[...] = jnp.zeros_like(total)
        ot[...] = jnp.zeros_like(ot)

        def forward(kb, _):
            values_t = vt[kb]
            for h in range(share):
                span = spans[h]
                p = jnp.exp2(kept[i, kb - i, :, span] * factor - top[:, span])
                kept[i, kb - i, :, span] = p
                total[:, span] += fold(p, jnp.sum)
                ot[:, span] += jnp.dot(
                    values_t, p.astype(jnp.bfloat16), preferred_element_type=jnp.float32
                )
            return 0

        lax.fori_loop(jnp.maximum(i, first_kb), i + reach, forward, 0)
        inverse = 1.0 / jnp.sum(total[...], 0, keepdims=True)
        out = ot[...] * inverse
        inv[i] = inverse
        delta[i] = jnp.sum(out * gt[i].astype(jnp.float32), 0, keepdims=True)
        for h in range(share):
            att[here, cols[h]] = out[:, spans[h]].T.astype(jnp.bfloat16)
        return 0

    lax.fori_loop(0, per_block, forward_tile, 0)
    att_swap = swap_out(4, att, q_cols, ao_ref)

    def back_slot(slot, _):
        @pl.when(block - (distance - slot) >= 0)
        def _():
            def key_step(t, _):
                kb = slot * per_block + t
                values = band[slot, 1, tile_rows(t), :]
                keys_t = kt[kb]

                def row_step(i, _):
                    here = tile_rows(i)
                    dv = jnp.zeros((TILE, HD), jnp.float32)
                    dk = jnp.zeros((TILE, HD), jnp.float32)
                    inverse, shift = inv[i], delta[i]
                    for h in range(share):
                        span = spans[h]
                        w = kept[i, kb - i, :, span] * inverse[:, span]
                        dp = jnp.dot(values, gt[i, :, span], preferred_element_type=jnp.float32)
                        ds = (w * (dp - shift[:, span])).astype(jnp.bfloat16)
                        dv += jnp.dot(
                            w.astype(jnp.bfloat16), go[here, cols[h]],
                            preferred_element_type=jnp.float32,
                        )
                        dk += jnp.dot(ds, qo[here, cols[h]], preferred_element_type=jnp.float32)
                        dqt[i, :, span] += jnp.dot(keys_t, ds, preferred_element_type=jnp.float32)
                    acc[0, tile_rows(kb), :] += dk
                    acc[1, tile_rows(kb), :] += dv
                    return 0

                lax.fori_loop(
                    jnp.maximum(kb - reach + 1, 0), jnp.minimum(kb + 1, per_block), row_step, 0
                )
                return 0

            lax.fori_loop(0, per_block, key_step, 0)
            whole = pl.ds(pl.multiple_of(slot * tokens, tokens), tokens)
            for c in range(2):
                by = scale if c == 0 else 1.0

                @pl.when((slot > 0) & has_next)
                def _():
                    hop_out(slot - 1, c).wait_recv()
                    both = acc[c, whole, :] * by + landed[slot - 1, c].astype(jnp.float32)
                    sums[slot, c] = both.astype(jnp.bfloat16)

                @pl.when(jnp.logical_not((slot > 0) & has_next))
                def _():
                    sums[slot, c] = (acc[c, whole, :] * by).astype(jnp.bfloat16)

            for c in range(2):
                @pl.when(slot < distance)
                def _():
                    hop_out(slot, c).start()

        return 0

    lax.fori_loop(0, distance + 1, back_slot, 0)

    def turn_back(i, _):
        for h in range(share):
            dq[tile_rows(i), cols[h]] = (dqt[i, :, spans[h]] * scale).T.astype(jnp.bfloat16)
        return 0

    lax.fori_loop(0, per_block, turn_back, 0)
    out_swaps = [
        swap_out(5, dq, q_cols, do_ref),
        swap_out(6, sums.at[distance, 0], HD, ko_ref),
        swap_out(7, sums.at[distance, 1], HD, vo_ref),
    ]
    for pair in kv_swap + qg_swap:
        for copy in pair[1]:
            copy.wait_send()
    for pair in [att_swap] + out_swaps:
        settle(pair)
        for copy in pair[1]:
            copy.wait_send()
    for c in range(2):
        for step in range(distance):
            @pl.when((block - step >= 0) & has_next)
            def _():
                hop_in(step, c).wait_send()

            @pl.when(block - (distance - step) >= 0)
            def _():
                hop_out(step, c).wait_send()


def per_device(queries, keys, values, grad_out, doc_ids):
    heads = lax.axis_size("head")
    peers = lax.axis_size("ctx")
    rows = queries.shape[0]
    group = keys.shape[1] // HD
    share = queries.shape[1] // HD // group
    ctx_low = group // heads
    blocks = peers // ctx_low
    tokens = rows * group
    distance = DOC_MOST // tokens
    bf16, f32 = jnp.bfloat16, jnp.float32
    vmem = pl.BlockSpec(memory_space=pltpu.VMEM)
    hbm = pl.BlockSpec(memory_space=pl.ANY)
    dma = pltpu.SemaphoreType.DMA
    base = lax.axis_index("ctx") // ctx_low * tokens
    padded = jnp.concatenate((jnp.full((distance * tokens,), -1, jnp.int32), doc_ids), 0)
    window = lax.dynamic_slice_in_dim(padded, base, (distance + 1) * tokens, 0)
    mine = lax.dynamic_slice_in_dim(doc_ids, base, tokens, 0)
    starts = base - distance * tokens + jnp.sum(
        (window[:, None] < mine[None, :]).astype(jnp.int32), 0, dtype=jnp.int32
    )
    tiles = tokens // TILE
    span = share * TILE
    all_tiles = (distance + 1) * tiles
    return pl.pallas_call(
        functools.partial(fused_kernel, heads, ctx_low, blocks, distance, HD ** -0.5),
        out_shape=(
            jax.ShapeDtypeStruct(queries.shape, bf16),
            jax.ShapeDtypeStruct(queries.shape, bf16),
            jax.ShapeDtypeStruct(keys.shape, bf16),
            jax.ShapeDtypeStruct(keys.shape, bf16),
        ),
        in_specs=[vmem] + [hbm] * 4,
        out_specs=(hbm,) * 4,
        scratch_shapes=[
            pltpu.VMEM((tokens, share * HD), bf16),
            pltpu.VMEM((tokens, share * HD), bf16),
            pltpu.VMEM((distance + 1, 2, tokens, HD), bf16),
            pltpu.VMEM((2, (distance + 1) * tokens, HD), f32),
            pltpu.VMEM((tiles, distance * tiles + 1, TILE, span), f32),
            pltpu.VMEM((tiles, HD, span), bf16),
            pltpu.VMEM((tiles, HD, span), bf16),
            pltpu.VMEM((tiles, 8, span), f32),
            pltpu.VMEM((8, span), f32),
            pltpu.VMEM((HD, span), f32),
            pltpu.VMEM((tiles, HD, span), f32),
            pltpu.VMEM((all_tiles, HD, TILE), bf16),
            pltpu.VMEM((all_tiles, HD, TILE), bf16),
            pltpu.VMEM((tiles, 1, span), f32),
            pltpu.VMEM((tiles, 1, span), f32),
            pltpu.VMEM((tokens, share * HD), bf16),
            pltpu.VMEM((tokens, share * HD), bf16),
            pltpu.VMEM((distance + 1, 2, tokens, HD), bf16),
            pltpu.VMEM((distance, 2, tokens, HD), bf16),
            dma((8,)), dma((8, group - 1)), dma((8, group - 1)),
            dma((distance, 2)), dma((distance, 2)), dma((distance, 2)), dma((distance, 2)),
        ],
        compiler_params=pltpu.CompilerParams(
            collective_id=1, has_side_effects=True, vmem_limit_bytes=67043328
        ),
        name="fused",
    )(starts.reshape(tiles, 1, TILE), queries, keys, values, grad_out)


def solution(mesh):
    spec = P(("ctx", "head"), None)
    return jax.shard_map(
        per_device,
        mesh=mesh,
        in_specs=(spec, spec, spec, spec, P()),
        out_specs=(spec, spec, spec, spec),
        check_vma=False,
    )
```

```python
import functools

import jax
import jax.numpy as jnp
from jax import lax
from jax.experimental import pallas as pl
from jax.experimental.pallas import tpu as pltpu
from jax.sharding import PartitionSpec as P

HD = 128
DOC_MOST = 2048
TILE = 256
LOG2E = 1.4426950408889634
MESH = pl.DeviceIdType.MESH


def place(ctx_low, heads):
    ctx, head = lax.axis_index("ctx"), lax.axis_index("head")
    block = ctx // ctx_low
    me = (ctx - block * ctx_low) * heads + head

    def member(number):
        return (block * ctx_low + number // heads, lax.rem(number, heads))

    return ctx, head, block, me, member


def greet(members, ctx, head, ctx_low, has_prev, has_next):
    barrier = pltpu.get_barrier_semaphore()
    for device in members:
        pl.semaphore_signal(barrier, inc=1, device_id=device, device_id_type=MESH)

    @pl.when(has_prev)
    def _():
        pl.semaphore_signal(barrier, inc=1, device_id=(ctx - ctx_low, head), device_id_type=MESH)

    @pl.when(has_next)
    def _():
        pl.semaphore_signal(barrier, inc=1, device_id=(ctx + ctx_low, head), device_id_type=MESH)

    near = has_prev.astype(jnp.int32) + has_next.astype(jnp.int32)
    pl.semaphore_wait(barrier, len(members) + near)


def fused_kernel(
    heads, ctx_low, blocks, distance, scale,
    start_ref, q_in, k_in, v_in, g_in,
    ao_ref, do_ref, ko_ref, vo_ref,
    qo, go, band, acc, kept, qt, gt, peak, total, ot, dqt, kt, vt, inv, delta,
    att, dq, sums, landed, wide,
    own_sem, send_sem, recv_sem, in_send, in_recv, out_send, out_recv,
):
    group = ctx_low * heads
    rows = q_in.shape[0]
    q_cols = q_in.shape[1] // group
    tokens = qo.shape[0]
    share = q_cols // HD
    factor = scale * LOG2E
    per_block = tokens // TILE
    reach = distance * per_block + 1
    ctx, head, block, me, member = place(ctx_low, heads)
    has_prev, has_next = block > 0, block < blocks - 1
    others = [lax.rem(me + step, group) for step in range(1, group)]
    greet([member(o) for o in others], ctx, head, ctx_low, has_prev, has_next)
    mine = pl.ds(pl.multiple_of(me * rows, rows), rows)
    base = block * tokens
    first_token = base - distance * tokens
    first_kb = jnp.maximum(distance - block, 0) * per_block

    def columns(width, number):
        return pl.ds(pl.multiple_of(number * width, width), width)

    def swap(a, pick_src, pick_dst):
        local = pltpu.make_async_copy(pick_src(me), pick_dst(me), own_sem.at[a])
        local.start()
        line = []
        for step, other in enumerate(others):
            copy = pltpu.make_async_remote_copy(
                src_ref=pick_src(other), dst_ref=pick_dst(me),
                send_sem=send_sem.at[a, step], recv_sem=recv_sem.at[a, step],
                device_id=member(other), device_id_type=MESH,
            )
            copy.start()
            line.append(copy)
        return local, line

    def swap_in(a, src, width, dst):
        return swap(a, lambda n: src.at[:, columns(width, n)], lambda n: dst.at[mine])

    def swap_out(a, src, width, dst):
        return swap(
            a,
            lambda n: src.at[pl.ds(pl.multiple_of(n * rows, rows), rows)],
            lambda n: dst.at[:, columns(width, n)],
        )

    def settle(pair):
        pair[0].wait()
        for copy in pair[1]:
            copy.wait_recv()

    def hop_in(step, c):
        return pltpu.make_async_remote_copy(
            src_ref=band.at[distance - step, c], dst_ref=band.at[distance - step - 1, c],
            send_sem=in_send.at[step, c], recv_sem=in_recv.at[step, c],
            device_id=(ctx + ctx_low, head), device_id_type=MESH,
        )

    def hop_out(step, c):
        return pltpu.make_async_remote_copy(
            src_ref=sums.at[step, c], dst_ref=landed.at[step, c],
            send_sem=out_send.at[step, c], recv_sem=out_recv.at[step, c],
            device_id=(ctx - ctx_low, head), device_id_type=MESH,
        )

    kv_swap = [
        swap_in(0, k_in, HD, band.at[distance, 0]),
        swap_in(1, v_in, HD, band.at[distance, 1]),
    ]
    qg_swap = [swap_in(2, q_in, q_cols, qo), swap_in(3, g_in, q_cols, go)]
    acc[...] = jnp.zeros_like(acc)
    dqt[...] = jnp.zeros_like(dqt)
    peak[...] = jnp.full_like(peak, -1e30)
    for c in range(2):
        settle(kv_swap[c])

        @pl.when(has_next)
        def _():
            hop_in(0, c).start()

    for pair in qg_swap:
        settle(pair)

    spans = [slice(h * TILE, (h + 1) * TILE) for h in range(share)]
    cols = [slice(h * HD, (h + 1) * HD) for h in range(share)]

    def tile_rows(i):
        return pl.ds(pl.multiple_of(i * TILE, TILE), TILE)

    def turn_rows(i, _):
        here = tile_rows(i)
        for h in range(share):
            qt[i, :, spans[h]] = qo[here, cols[h]].T
            gt[i, :, spans[h]] = go[here, cols[h]].T
        return 0

    lax.fori_loop(0, per_block, turn_rows, 0)

    def across(x, y):
        return lax.dot_general(
            x, y, (((1,), (1,)), ((), ())), preferred_element_type=jnp.float32
        )

    def fold(x, op):
        return op(x.reshape(TILE // 8, 8, TILE), 0)

    def score_slot(n, _):
        slot = distance - n

        @pl.when(block - n >= 0)
        def _():
            for c in range(2):
                @pl.when(n > 0)
                def _():
                    hop_in(n - 1, c).wait_recv()

                @pl.when((n > 0) & (n < distance) & has_next)
                def _():
                    hop_in(n, c).start()

            def key_step(t, _):
                kb = slot * per_block + t
                here = tile_rows(t)
                keys = band[slot, 0, here, :]
                kt[kb] = keys.T
                vt[kb] = band[slot, 1, here, :].T
                tile_token = first_token + kb * TILE
                col = tile_token + lax.broadcasted_iota(jnp.int32, (TILE, TILE), 0)

                def row_step(i, _):
                    starts = start_ref[i]
                    token = base + i * TILE + lax.broadcasted_iota(jnp.int32, (TILE, TILE), 1)
                    seen = (col >= starts) & (col <= token)
                    for h in range(share):
                        s = jnp.dot(keys, qt[i, :, spans[h]], preferred_element_type=jnp.float32)
                        s = jnp.where(seen, s, -1e30)
                        kept[i, kb - i, :, spans[h]] = s
                        peak[i, :, spans[h]] = jnp.maximum(peak[i, :, spans[h]], fold(s, jnp.max))
                    return 0

                lax.fori_loop(
                    jnp.maximum(kb - reach + 1, 0), jnp.minimum(kb + 1, per_block), row_step, 0
                )
                return 0

            lax.fori_loop(0, per_block, key_step, 0)

        return 0

    lax.fori_loop(0, distance + 1, score_slot, 0)

    def forward_tile(i, _):
        here = tile_rows(i)
        top = jnp.max(peak[i], 0, keepdims=True) * factor
        total[...] = jnp.zeros_like(total)
        ot[...] = jnp.zeros_like(ot)

        def forward(kb, _):
            values_t = vt[kb]
            for h in range(share):
                span = spans[h]
                p = jnp.exp2(kept[i, kb - i, :, span] * factor - top[:, span])
                kept[i, kb - i, :, span] = p
                total[:, span] += fold(p, jnp.sum)
                ot[:, span] += jnp.dot(
                    values_t, p.astype(jnp.bfloat16), preferred_element_type=jnp.float32
                )
            return 0

        lax.fori_loop(jnp.maximum(i, first_kb), i + reach, forward, 0)
        inverse = 1.0 / jnp.sum(total[...], 0, keepdims=True)
        out = ot[...] * inverse
        inv[i] = inverse
        delta[i] = jnp.sum(out * gt[i].astype(jnp.float32), 0, keepdims=True)
        for h in range(share):
            att[here, cols[h]] = out[:, spans[h]].T.astype(jnp.bfloat16)
        return 0

    lax.fori_loop(0, per_block, forward_tile, 0)
    att_swap = swap_out(4, att, q_cols, ao_ref)

    def back_slot(slot, _):
        @pl.when(block - (distance - slot) >= 0)
        def _():
            def key_step(t, _):
                kb = slot * per_block + t
                values = band[slot, 1, tile_rows(t), :]
                keys_t = kt[kb]

                def row_step(i, _):
                    inverse, shift = inv[i], delta[i]
                    for h in range(share):
                        span = spans[h]
                        w = kept[i, kb - i, :, span] * inverse[:, span]
                        dp = jnp.dot(values, gt[i, :, span], preferred_element_type=jnp.float32)
                        wide[0, :, span] = w.astype(jnp.bfloat16)
                        wide[1, :, span] = (w * (dp - shift[:, span])).astype(jnp.bfloat16)
                    dqt[i] += jnp.dot(keys_t, wide[1], preferred_element_type=jnp.float32)
                    dv = across(gt[i], wide[0])
                    dk = across(qt[i], wide[1])
                    acc[0, kb] += dk
                    acc[1, kb] += dv
                    return 0

                lax.fori_loop(
                    jnp.maximum(kb - reach + 1, 0), jnp.minimum(kb + 1, per_block), row_step, 0
                )
                return 0

            lax.fori_loop(0, per_block, key_step, 0)
            for c in range(2):
                by = scale if c == 0 else 1.0

                def term(t):
                    return (acc[c, slot * per_block + t] * by).T

                @pl.when((slot > 0) & has_next)
                def _():
                    hop_out(slot - 1, c).wait_recv()
                    for t in range(per_block):
                        rows_t = slice(t * TILE, (t + 1) * TILE)
                        both = term(t) + landed[slot - 1, c, rows_t, :].astype(jnp.float32)
                        sums[slot, c, rows_t, :] = both.astype(jnp.bfloat16)

                @pl.when(jnp.logical_not((slot > 0) & has_next))
                def _():
                    for t in range(per_block):
                        sums[slot, c, t * TILE:(t + 1) * TILE, :] = term(t).astype(jnp.bfloat16)

            for c in range(2):
                @pl.when(slot < distance)
                def _():
                    hop_out(slot, c).start()

        return 0

    lax.fori_loop(0, distance + 1, back_slot, 0)

    def turn_back(i, _):
        for h in range(share):
            dq[tile_rows(i), cols[h]] = (dqt[i, :, spans[h]] * scale).T.astype(jnp.bfloat16)
        return 0

    lax.fori_loop(0, per_block, turn_back, 0)
    out_swaps = [
        swap_out(5, dq, q_cols, do_ref),
        swap_out(6, sums.at[distance, 0], HD, ko_ref),
        swap_out(7, sums.at[distance, 1], HD, vo_ref),
    ]
    for pair in kv_swap + qg_swap:
        for copy in pair[1]:
            copy.wait_send()
    for pair in [att_swap] + out_swaps:
        settle(pair)
        for copy in pair[1]:
            copy.wait_send()
    for c in range(2):
        for step in range(distance):
            @pl.when((block - step >= 0) & has_next)
            def _():
                hop_in(step, c).wait_send()

            @pl.when(block - (distance - step) >= 0)
            def _():
                hop_out(step, c).wait_send()


def per_device(queries, keys, values, grad_out, doc_ids):
    heads = lax.axis_size("head")
    peers = lax.axis_size("ctx")
    rows = queries.shape[0]
    group = keys.shape[1] // HD
    share = queries.shape[1] // HD // group
    ctx_low = group // heads
    blocks = peers // ctx_low
    tokens = rows * group
    distance = DOC_MOST // tokens
    bf16, f32 = jnp.bfloat16, jnp.float32
    vmem = pl.BlockSpec(memory_space=pltpu.VMEM)
    hbm = pl.BlockSpec(memory_space=pl.ANY)
    dma = pltpu.SemaphoreType.DMA
    base = lax.axis_index("ctx") // ctx_low * tokens
    padded = jnp.concatenate((jnp.full((distance * tokens,), -1, jnp.int32), doc_ids), 0)
    window = lax.dynamic_slice_in_dim(padded, base, (distance + 1) * tokens, 0)
    mine = lax.dynamic_slice_in_dim(doc_ids, base, tokens, 0)
    starts = base - distance * tokens + jnp.sum(
        (window[:, None] < mine[None, :]).astype(jnp.int32), 0, dtype=jnp.int32
    )
    tiles = tokens // TILE
    span = share * TILE
    all_tiles = (distance + 1) * tiles
    return pl.pallas_call(
        functools.partial(fused_kernel, heads, ctx_low, blocks, distance, HD ** -0.5),
        out_shape=(
            jax.ShapeDtypeStruct(queries.shape, bf16),
            jax.ShapeDtypeStruct(queries.shape, bf16),
            jax.ShapeDtypeStruct(keys.shape, bf16),
            jax.ShapeDtypeStruct(keys.shape, bf16),
        ),
        in_specs=[vmem] + [hbm] * 4,
        out_specs=(hbm,) * 4,
        scratch_shapes=[
            pltpu.VMEM((tokens, share * HD), bf16),
            pltpu.VMEM((tokens, share * HD), bf16),
            pltpu.VMEM((distance + 1, 2, tokens, HD), bf16),
            pltpu.VMEM((2, all_tiles, HD, TILE), f32),
            pltpu.VMEM((tiles, distance * tiles + 1, TILE, span), f32),
            pltpu.VMEM((tiles, HD, span), bf16),
            pltpu.VMEM((tiles, HD, span), bf16),
            pltpu.VMEM((tiles, 8, span), f32),
            pltpu.VMEM((8, span), f32),
            pltpu.VMEM((HD, span), f32),
            pltpu.VMEM((tiles, HD, span), f32),
            pltpu.VMEM((all_tiles, HD, TILE), bf16),
            pltpu.VMEM((all_tiles, HD, TILE), bf16),
            pltpu.VMEM((tiles, 1, span), f32),
            pltpu.VMEM((tiles, 1, span), f32),
            pltpu.VMEM((tokens, share * HD), bf16),
            pltpu.VMEM((tokens, share * HD), bf16),
            pltpu.VMEM((distance + 1, 2, tokens, HD), bf16),
            pltpu.VMEM((distance, 2, tokens, HD), bf16),
            pltpu.VMEM((2, TILE, span), bf16),
            dma((8,)), dma((8, group - 1)), dma((8, group - 1)),
            dma((distance, 2)), dma((distance, 2)), dma((distance, 2)), dma((distance, 2)),
        ],
        compiler_params=pltpu.CompilerParams(
            collective_id=1, has_side_effects=True, vmem_limit_bytes=67043328
        ),
        name="fused",
    )(starts.reshape(tiles, 1, TILE), queries, keys, values, grad_out)


def solution(mesh):
    spec = P(("ctx", "head"), None)
    return jax.shard_map(
        per_device,
        mesh=mesh,
        in_specs=(spec, spec, spec, spec, P()),
        out_specs=(spec, spec, spec, spec),
        check_vma=False,
    )
```
